32 devices in a mesh: dp: 8 (over y, x, core), stream: 4 (over z).
Axes of the slice: x: 2, y: 2, z: 4, core: 2. Of those that a mesh axis runs over, the one named last changes fastest.
Arguments:
- main_states: bfloat16 [4096, 1024], P(('dp', 'stream')), may hold values from -12 to 12
- predict_states: bfloat16 [2, 4096, 1024], P(None, ('dp', 'stream')), may hold values from -6 to 6
- encoder_states: bfloat16 [4096, 1024], P(('dp', 'stream')), may hold values from -12 to 12
- doc_lengths: int32 [8, 8], P('dp'), may hold values from 0 to 512, as said below
- encoder_keep: int32 [4096], P('dp'), may hold values 0 or 1
- bucket_table: int32 [512], replicated, may hold values from 0 to 31, as said below
- query_weight: bfloat16 [1024, 1024], replicated, may hold values from -0.1875 to 0.1875
- key_weight: bfloat16 [1024, 1024], replicated, may hold values from -0.1875 to 0.1875
- value_weight: bfloat16 [1024, 1024], replicated, may hold values from -0.1875 to 0.1875
- out_weight: bfloat16 [1024, 1024], replicated, may hold values from -0.5 to 0.5
- cross_query_weight: bfloat16 [1024, 1024], replicated, may hold values from -0.1875 to 0.1875
- cross_key_weight: bfloat16 [1024, 1024], replicated, may hold values from -0.1875 to 0.1875
- cross_value_weight: bfloat16 [1024, 1024], replicated, may hold values from -0.1875 to 0.1875
- cross_out_weight: bfloat16 [1024, 1024], replicated, may hold values from -0.5 to 0.5
- up_weight: bfloat16 [1024, 4096], replicated, may hold values from -0.1875 to 0.1875
- down_weight: bfloat16 [4096, 1024], replicated, may hold values from -0.09375 to 0.09375
- relative_bias: bfloat16 [32, 16], replicated, may hold values from -6 to 6
- query_bias: float32 [1024], replicated, may hold values from -1.75 to 1.75
- value_bias: float32 [1024], replicated, may hold values from -1.75 to 1.75
- out_bias: float32 [1024], replicated, may hold values from -1.75 to 1.75
- cross_query_bias: float32 [1024], replicated, may hold values from -1.75 to 1.75
- cross_value_bias: float32 [1024], replicated, may hold values from -1.75 to 1.75
- cross_out_bias: float32 [1024], replicated, may hold values from -1.75 to 1.75
- up_bias: float32 [4096], replicated, may hold values from -1.75 to 1.75
- down_bias: float32 [1024], replicated, may hold values from -1.75 to 1.75
- norm_gain: float32 [3, 1024], replicated, may hold values from 0.5 to 1.5
- norm_shift: float32 [3, 1024], replicated, may hold values from -1.75 to 1.75
- main_cotangent: bfloat16 [4096, 1024], P(('dp', 'stream')), may hold values from -6 to 6
- predict_cotangent: bfloat16 [2, 4096, 1024], P(None, ('dp', 'stream')), may hold values from -6 to 6
Outputs:
- main_out: bfloat16 [4096, 1024], P(('dp', 'stream'))
- predict_out: bfloat16 [2, 4096, 1024], P(None, ('dp', 'stream'))
- main_grad: bfloat16 [4096, 1024], P(('dp', 'stream'))
- predict_grad: bfloat16 [2, 4096, 1024], P(None, ('dp', 'stream'))
- encoder_grad: bfloat16 [4096, 1024], P(('dp', 'stream'))
- query_weight_grad: float32 [1024, 1024], P('dp', 'stream')
- key_weight_grad: float32 [1024, 1024], P('dp', 'stream')
- value_weight_grad: float32 [1024, 1024], P('dp', 'stream')
- out_weight_grad: float32 [1024, 1024], P('dp', 'stream')
- cross_query_weight_grad: float32 [1024, 1024], P('dp', 'stream')
- cross_key_weight_grad: float32 [1024, 1024], P('dp', 'stream')
- cross_value_weight_grad: float32 [1024, 1024], P('dp', 'stream')
- cross_out_weight_grad: float32 [1024, 1024], P('dp', 'stream')
- up_weight_grad: float32 [1024, 4096], P('dp', 'stream')
- down_weight_grad: float32 [4096, 1024], P('dp', 'stream')
- relative_bias_grad: float32 [32, 16], replicated
- query_bias_grad: float32 [1024], replicated
- value_bias_grad: float32 [1024], replicated
- out_bias_grad: float32 [1024], replicated
- cross_query_bias_grad: float32 [1024], replicated
- cross_value_bias_grad: float32 [1024], replicated
- cross_out_bias_grad: float32 [1024], replicated
- up_bias_grad: float32 [4096], replicated
- down_bias_grad: float32 [1024], replicated
- norm_gain_grad: float32 [3, 1024], replicated
- norm_shift_grad: float32 [3, 1024], replicated
The draws below stay inside these ranges and needn't reach their ends.
Inputs may be any that keep to these rules, and one draw needn't show every extreme that they name: `doc_lengths`: slot j of a buffer holds the length of its j-th document, 64 to 512 tokens, or 0 once the buffer's documents are over; a buffer's lengths sum to at most 512, and its first slot is never 0. `bucket_table`: entry d is the bucket of distance d; it never falls as d grows, and entry 0 is 0.
All inputs are finite; a program needn't handle non-finite values. No bound on the sum of `encoder_keep` on one device may be relied on, other than what follows from the above.
Results may differ from the reference program's by a relative error of at most 0.025.
Values may be sent and summed in bfloat16 or wider, within the bound.
No kernel may reach another device: no remote copies, remote signals or barrier semaphores. Data moves between devices by JAX's collectives and lax.ppermute only.
A program may use at most 256 MiB of HBM per device.

```python
import jax
import jax.numpy as jnp
from jax import lax

D = 1024
HEADS = 16
HEAD = 64
FF = 4096
NGRAM = 2
BUCKETS = 32
DOCS = 8
DOC_MIN = 64
DOC_MAX = 512
CAP = 512
TOKENS = 4096
N_DP = 8


def draw_doc_lengths(key, part):
    drawn = jax.random.randint(key, (N_DP, DOCS), DOC_MIN, DOC_MAX + 1).astype(jnp.int32)
    first_slot = (jnp.arange(N_DP)[:, None] == 0) & (jnp.arange(DOCS)[None, :] == 0)
    drawn = jnp.where(first_slot, DOC_MAX, drawn).astype(jnp.int32)
    doc_ends = jnp.cumsum(drawn, axis=1).astype(jnp.int32)
    return jnp.where(doc_ends <= CAP, drawn, 0).astype(jnp.int32)


def draw_bucket_table(key, part):
    shuffled = jax.random.permutation(key, CAP - 1).astype(jnp.int32) + 1
    marks = shuffled[:BUCKETS - 1]
    places = jnp.arange(CAP, dtype=jnp.int32)
    return jnp.sum((marks[None, :] <= places[:, None]).astype(jnp.int32), axis=1).astype(jnp.int32)


def plant(values, stream_key, least, largest):
    extent = values.shape
    index_at = [jax.random.randint(jax.random.fold_in(stream_key, axis), (), 0, extent[axis]) for axis in range(len(extent))]
    values = values.at[tuple(index_at)].set(least)
    longest = extent.index(max(extent))
    index_at[longest] = (index_at[longest] + 1) % extent[longest]
    return values.at[tuple(index_at)].set(largest)


def with_spikes(values, stream_key, source, target, shards_of, factor):
    def block_of(position):
        return (jnp.arange(values.shape[position]) // (values.shape[position] // shards_of)).reshape((-1,) + (1,) * (values.ndim - 1 - position))

    near = jax.random.permutation(stream_key, shards_of)[block_of(target)]
    second = (block_of(target) + shards_of // 2) % shards_of
    return jnp.where((block_of(source) == near) | (block_of(source) == second), factor * values, values)


def block_levels(stream_key, dims, cuts, smallest, high):
    loudness = 1.0
    for axis_at, shards_of in cuts:
        heights = jax.random.uniform(jax.random.fold_in(jax.random.fold_in(stream_key, 6), axis_at), (shards_of,), jnp.float32, smallest / len(cuts), high / len(cuts))
        loudness = loudness * jnp.repeat(jnp.exp(heights), dims[axis_at] // shards_of).reshape((-1,) + (1,) * (len(dims) - 1 - axis_at))
    return loudness


def noise(stream_key, extent, width, limit, shards=(), kind=jnp.bfloat16):
    values = width * jax.random.normal(stream_key, extent, jnp.float32)
    if shards:
        values = values * block_levels(stream_key, extent, shards, -0.22, 0.18)
    return jnp.clip(values, -limit, limit).astype(kind)


def bell_draw_with(own_key, extent, scale, limit, split, heavy, kind=jnp.bfloat16):
    entries = scale * jax.random.normal(own_key, extent, jnp.float32)
    if split:
        entries = entries * block_levels(own_key, extent, split, -0.22, 0.18)
    return jnp.clip(with_spikes(entries, jax.random.fold_in(own_key, 3), *heavy), -limit, limit).astype(kind)


def setup_inputs(seed: int = 0) -> dict:
    seeds = jax.random.split(jax.random.key(seed), 30)
    return {
        "main_states": bell_draw_with(seeds[0], (TOKENS, D), 1.0, 12.0, ((0, 32),), (0, 1, 32, 2.75)),
        "predict_states": noise(seeds[1], (NGRAM, TOKENS, D), 1.0, 6.0, ((1, 32),)),
        "encoder_states": bell_draw_with(seeds[2], (TOKENS, D), 1.0, 12.0, ((0, 32),), (0, 1, 32, 2.75)),
        "doc_lengths": draw_doc_lengths(jax.random.fold_in(seeds[29], 71), 0),
        "encoder_keep": plant((jax.random.randint(seeds[4], (TOKENS,), 0, 8) < 7).astype(jnp.int32), jax.random.fold_in(seeds[4], 1), 0, 1),
        "bucket_table": draw_bucket_table(jax.random.fold_in(seeds[29], 71), 0),
        "query_weight": noise(seeds[6], (D, D), D ** -0.5, 0.1875),
        "key_weight": noise(seeds[7], (D, D), D ** -0.5, 0.1875),
        "value_weight": noise(seeds[8], (D, D), D ** -0.5, 0.1875),
        "out_weight": noise(seeds[9], (D, D), (D // 8) ** -0.5, 0.5),
        "cross_query_weight": noise(seeds[10], (D, D), D ** -0.5, 0.1875),
        "cross_key_weight": noise(seeds[11], (D, D), D ** -0.5, 0.1875),
        "cross_value_weight": noise(seeds[12], (D, D), D ** -0.5, 0.1875),
        "cross_out_weight": noise(seeds[13], (D, D), (D // 8) ** -0.5, 0.5),
        "up_weight": noise(seeds[14], (D, FF), D ** -0.5, 0.1875),
        "down_weight": noise(seeds[15], (FF, D), FF ** -0.5, 0.09375),
        "relative_bias": noise(seeds[16], (BUCKETS, HEADS), 1.0, 6.0),
        "query_bias": noise(seeds[17], (D,), 0.3, 1.75, (), jnp.float32),
        "value_bias": noise(seeds[18], (D,), 0.3, 1.75, (), jnp.float32),
        "out_bias": noise(seeds[19], (D,), 0.3, 1.75, (), jnp.float32),
        "cross_query_bias": noise(seeds[20], (D,), 0.3, 1.75, (), jnp.float32),
        "cross_value_bias": noise(seeds[21], (D,), 0.3, 1.75, (), jnp.float32),
        "cross_out_bias": noise(seeds[22], (D,), 0.3, 1.75, (), jnp.float32),
        "up_bias": noise(seeds[23], (FF,), 0.3, 1.75, (), jnp.float32),
        "down_bias": noise(seeds[24], (D,), 0.3, 1.75, (), jnp.float32),
        "norm_gain": jnp.clip(1.0 + 0.1 * jax.random.normal(seeds[25], (3, D), jnp.float32), 0.5, 1.5),
        "norm_shift": noise(seeds[26], (3, D), 0.3, 1.75, (), jnp.float32),
        "main_cotangent": noise(seeds[27], (TOKENS, D), 1.0, 6.0, ((0, 32),)),
        "predict_cotangent": noise(seeds[28], (NGRAM, TOKENS, D), 1.0, 6.0, ((1, 32),)),
    }


@jax.custom_vjp
def low(v):
    return lax.optimization_barrier(v.astype(jnp.bfloat16)).astype(jnp.float32)

@jax.custom_vjp
def low_back(v):
    return v

def low_keep(v):
    return (low(v), None)

def low_pass(kept, grad):
    return (grad,)

def back_keep(v):
    return (v, None)

def back_low(kept, grad):
    return (low(grad),)
low.defvjp(low_keep, low_pass)
low_back.defvjp(back_keep, back_low)
EPS = 1e-05
BIG = -1e+30
HIGHEST = lax.Precision.HIGHEST

def matmul(left, right):
    return jnp.dot(left, right, precision=HIGHEST, preferred_element_type=jnp.float32)

def norm_rows(resid, gain, shift):
    centre = lax.optimization_barrier(jnp.mean(resid, axis=-1, keepdims=True))
    centred = resid - centre
    spread = lax.optimization_barrier(jnp.mean(centred * centred, axis=-1, keepdims=True))
    return centred * lax.rsqrt(spread + EPS) * gain + shift

def group_heads(array):
    return array.reshape(NGRAM + 1, CAP, HEADS, HEAD)

def enc_heads(array):
    return array.reshape(CAP, HEADS, HEAD)

def layer_block(main, predict, encoder, lengths, keep_in, table, params):
    query_weight, key_weight, value_weight, out_weight, cross_query_weight, cross_key_weight, cross_value_weight, cross_out_weight, up_weight, down_weight, relative_bias, query_bias, value_bias, out_bias, cross_query_bias, cross_value_bias, cross_out_bias, up_bias, down_bias, norm_gain, norm_shift = params
    doc_ends = jnp.cumsum(lengths).astype(jnp.int32)
    places = jnp.arange(CAP, dtype=jnp.int32)
    segment = lax.optimization_barrier(jnp.sum((doc_ends[None, :] <= places[:, None]).astype(jnp.int32), axis=1)).astype(jnp.int32)
    earlier = jnp.concatenate([jnp.full((1,), -1, jnp.int32), segment[:-1]])
    usable = (keep_in > 0) | (segment != earlier)
    same_doc = segment[:, None] == segment[None, :]
    causal = places[None, :] <= places[:, None]
    before = places[None, :] < places[:, None]
    self_mask = jnp.stack([same_doc & causal] + [same_doc & before] * NGRAM)[:, None]
    own_ok = jnp.broadcast_to((jnp.arange(NGRAM + 1) > 0)[:, None, None, None], (NGRAM + 1, 1, CAP, 1))
    full_mask = jnp.concatenate([jnp.broadcast_to(self_mask, (NGRAM + 1, 1, CAP, CAP)), own_ok], axis=-1)
    cross_mask = (same_doc & usable[None, :])[None, None]
    distance = jnp.clip(places[:, None] - places[None, :], 0, CAP - 1).astype(jnp.int32)
    bias = jnp.transpose(relative_bias[table[distance]], (2, 0, 1))
    own_bias = relative_bias[table[0]]
    factor = HEAD ** (-0.5)
    rows = jnp.concatenate([main[None], predict], axis=0)
    queries = low_back(low(matmul(rows, query_weight) + query_bias))
    keys = low_back(low(matmul(rows, key_weight)))
    values = low_back(low(matmul(rows, value_weight) + value_bias))
    query_heads = group_heads(queries)
    key_group = group_heads(keys)
    value_group = group_heads(values)
    scores = jnp.einsum('gthd,shd->ghts', query_heads, key_group[0], precision=HIGHEST) * factor + bias[None]
    own_scores = jnp.einsum('gthd,gthd->ght', query_heads, key_group, precision=HIGHEST) * factor + own_bias[None, :, None]
    every_score = low_back(jnp.concatenate([scores, own_scores[..., None]], axis=-1))
    weights = low(jax.nn.softmax(jnp.where(full_mask, every_score, BIG), axis=-1))
    attended = jnp.einsum('ghts,shd->gthd', weights[..., :CAP], value_group[0], precision=HIGHEST)
    attended = attended + jnp.transpose(weights[..., CAP], (0, 2, 1))[..., None] * value_group
    attended = low_back(low(attended.reshape(NGRAM + 1, CAP, D)))
    branch = low_back(matmul(attended, out_weight) + out_bias)
    hidden_one = norm_rows(rows + branch, norm_gain[0], norm_shift[0])
    cross_queries = low_back(low(matmul(low(hidden_one), cross_query_weight) + cross_query_bias))
    cross_keys = low_back(low(matmul(encoder, cross_key_weight)))
    cross_values = low_back(low(matmul(encoder, cross_value_weight) + cross_value_bias))
    cross_scores = jnp.einsum('gthd,shd->ghts', group_heads(cross_queries), enc_heads(cross_keys), precision=HIGHEST) * factor
    cross_scores = low_back(cross_scores)
    cross_weights = low(jax.nn.softmax(jnp.where(cross_mask, cross_scores, BIG), axis=-1))
    cross_attended = jnp.einsum('ghts,shd->gthd', cross_weights, enc_heads(cross_values), precision=HIGHEST)
    cross_attended = low_back(low(cross_attended.reshape(NGRAM + 1, CAP, D)))
    cross_branch = low_back(matmul(cross_attended, cross_out_weight) + cross_out_bias)
    hidden_two = norm_rows(hidden_one + cross_branch, norm_gain[1], norm_shift[1])
    inner = low_back(matmul(low(hidden_two), up_weight) + up_bias)
    activated = low(jax.nn.gelu(inner, approximate=False))
    ffn_out = low_back(matmul(activated, down_weight) + down_bias)
    return norm_rows(hidden_two + ffn_out, norm_gain[2], norm_shift[2])

def reference(main_states, predict_states, encoder_states, doc_lengths, encoder_keep, bucket_table, query_weight, key_weight, value_weight, out_weight, cross_query_weight, cross_key_weight, cross_value_weight, cross_out_weight, up_weight, down_weight, relative_bias, query_bias, value_bias, out_bias, cross_query_bias, cross_value_bias, cross_out_bias, up_bias, down_bias, norm_gain, norm_shift, main_cotangent, predict_cotangent):
    params = tuple((weight.astype(jnp.float32) for weight in (query_weight, key_weight, value_weight, out_weight, cross_query_weight, cross_key_weight, cross_value_weight, cross_out_weight, up_weight, down_weight, relative_bias, query_bias, value_bias, out_bias, cross_query_bias, cross_value_bias, cross_out_bias, up_bias, down_bias, norm_gain, norm_shift)))
    main = main_states.astype(jnp.float32).reshape(N_DP, CAP, D)
    predict = jnp.transpose(predict_states.astype(jnp.float32).reshape(NGRAM, N_DP, CAP, D), (1, 0, 2, 3))
    encoder = encoder_states.astype(jnp.float32).reshape(N_DP, CAP, D)
    keep_in = encoder_keep.reshape(N_DP, CAP)

    def forward(main_rows, predict_rows, encoder_rows, weights):

        def one_buffer(item):
            return layer_block(item[0], item[1], item[2], item[3], item[4], bucket_table, weights)
        return lax.map(jax.checkpoint(one_buffer), (main_rows, predict_rows, encoder_rows, doc_lengths, keep_in))
    outputs, pull = jax.vjp(forward, main, predict, encoder, params)
    used = lax.optimization_barrier(jnp.sum(doc_lengths, axis=1)).astype(jnp.int32)
    live = (jnp.arange(CAP, dtype=jnp.int32)[None, :] < used[:, None]).astype(jnp.float32)
    cotangent = jnp.concatenate([main_cotangent.reshape(N_DP, 1, CAP, D), jnp.transpose(predict_cotangent.reshape(NGRAM, N_DP, CAP, D), (1, 0, 2, 3))], axis=1).astype(jnp.float32)
    cotangent = cotangent * live[:, None, :, None]
    main_back, predict_back, encoder_back, weight_back = pull(cotangent)
    main_out = outputs[:, 0].reshape(TOKENS, D).astype(jnp.bfloat16)
    predict_out = jnp.transpose(outputs[:, 1:], (1, 0, 2, 3)).reshape(NGRAM, TOKENS, D).astype(jnp.bfloat16)
    main_grad = main_back.reshape(TOKENS, D).astype(jnp.bfloat16)
    predict_grad = jnp.transpose(predict_back, (1, 0, 2, 3)).reshape(NGRAM, TOKENS, D).astype(jnp.bfloat16)
    encoder_grad = encoder_back.reshape(TOKENS, D).astype(jnp.bfloat16)
    return (main_out, predict_out, main_grad, predict_grad, encoder_grad, weight_back[0], weight_back[1], weight_back[2], weight_back[3], weight_back[4], weight_back[5], weight_back[6], weight_back[7], weight_back[8], weight_back[9], weight_back[10], weight_back[11], weight_back[12], weight_back[13], weight_back[14], weight_back[15], weight_back[16], weight_back[17], weight_back[18], weight_back[19], weight_back[20])
```

```python
import functools
import jax
import jax.numpy as jnp
from jax import lax
from jax.sharding import PartitionSpec as P
from jax.experimental import pallas as pl
from jax.experimental.pallas import tpu as pltpu

F32 = jnp.float32
BF16 = jnp.bfloat16
BIG = -1e30
HEAD = 64


def dot_nt(left, right):
    return lax.dot_general(left, right, (((1,), (1,)), ((), ())), preferred_element_type=F32)


def dot_nn(left, right):
    return lax.dot_general(left, right, (((1,), (0,)), ((), ())), preferred_element_type=F32)


def head_mask(which):
    lane = lax.broadcasted_iota(jnp.int32, (1, 2 * HEAD), 1)
    return ((lane // HEAD) == which).astype(F32).astype(BF16)


def flip(array):
    return array.astype(F32).T


def self_masks(ends_ref, mask_sc, blocks, rows):
    for block in range(blocks):
        key_at, row_at, same = segment_same(ends_ref, block, blocks, rows)
        at = pl.ds(block * rows, rows)
        mask_sc[0, at, :] = jnp.where(same & (key_at <= row_at), 0.0, BIG)
        mask_sc[1, at, :] = jnp.where(same & (key_at < row_at), 0.0, BIG)


def segment_same(ends_ref, block, blocks, rows):
    slots = ends_ref.shape[0] - 1 - blocks
    key_at = lax.broadcasted_iota(jnp.int32, (rows, rows), 0) + ends_ref[slots + 1 + block]
    row_at = lax.broadcasted_iota(jnp.int32, (rows, rows), 1) + ends_ref[slots]
    key_seg = jnp.zeros((rows, rows), jnp.int32)
    row_seg = jnp.zeros((rows, rows), jnp.int32)
    for slot in range(slots):
        end = ends_ref[slot]
        key_seg = key_seg + (key_at >= end).astype(jnp.int32)
        row_seg = row_seg + (row_at >= end).astype(jnp.int32)
    return key_at, row_at, key_seg == row_seg


def toeplitz(vec_ref, which, blocks, rows):
    parts = []
    for block in range(blocks):
        line = vec_ref[0, which, block : block + 1, :]
        wide = jnp.broadcast_to(line, (rows, 2 * rows))
        parts.append(pltpu.roll(wide, 0, axis=1, stride=1, stride_axis=0)[:, :rows])
    return jnp.concatenate(parts, axis=0)


def self_fwd_kernel(
    ends_ref, own_bias_ref, q_ref, k_ref, v_ref, ok_ref, ov_ref, vec_ref, out_ref, lse_ref, mask_sc
):
    groups, rows, _ = q_ref.shape
    keys = k_ref.shape[0]
    pair = pl.program_id(0)

    @pl.when(pair == 0)
    def _():
        self_masks(ends_ref, mask_sc, keys // rows, rows)

    queries = q_ref[...].reshape(groups * rows, 2 * HEAD) * jnp.asarray(0.125, BF16)
    keyset = k_ref[...]
    value_t = flip(v_ref[...]).astype(BF16)
    query_t = [flip(queries[g * rows : (g + 1) * rows]) for g in range(1, groups)]
    own_key_t = [flip(ok_ref[g]) for g in range(groups - 1)]
    own_value_t = [flip(ov_ref[g]) for g in range(groups - 1)]
    own_prod = [a * b for a, b in zip(query_t, own_key_t)]
    outs = []
    for which in range(2):
        lo, hi = which * HEAD, (which + 1) * HEAD
        scores = dot_nt(keyset, queries * head_mask(which))
        bias = toeplitz(vec_ref, which, keys // rows, rows)
        bias_main = bias + mask_sc[0]
        bias_copy = bias + mask_sc[1]
        head_out = []
        for g in range(groups):
            logit = scores[:, g * rows : (g + 1) * rows] + (bias_main if g == 0 else bias_copy)
            top = jnp.max(logit, axis=0, keepdims=True)
            if g:
                own_logit = (
                    jnp.sum(own_prod[g - 1][lo:hi], axis=0, keepdims=True)
                    + own_bias_ref[2 * pair + which]
                )
                top = jnp.maximum(top, own_logit)
            expon = jnp.exp(logit - top)
            total = jnp.sum(expon, axis=0, keepdims=True)
            result = dot_nn(value_t[lo:hi], expon.astype(BF16))
            if g:
                own_exp = jnp.exp(own_logit - top)
                total = total + own_exp
                result = result + own_exp * own_value_t[g - 1][lo:hi]
            head_out.append(result / total)
            lse_ref[0, which : which + 1, g * rows : (g + 1) * rows] = top + jnp.log(total)
        outs.append(head_out)
    for g in range(groups):
        both = jnp.concatenate([outs[0][g], outs[1][g]], axis=0)
        out_ref[g] = both.T.astype(BF16)


def self_bwd_kernel(
    ends_ref,
    own_bias_ref,
    q_ref,
    k_ref,
    v_ref,
    ok_ref,
    ov_ref,
    vec_ref,
    lse_ref,
    do_ref,
    dq_ref,
    dk_ref,
    dv_ref,
    dok_ref,
    dov_ref,
    diag_ref,
    own_ref,
    mask_sc,
):
    groups, rows, _ = q_ref.shape
    keys = k_ref.shape[0]
    blocks = keys // rows
    pair = pl.program_id(0)

    @pl.when(pair == 0)
    def _():
        self_masks(ends_ref, mask_sc, keys // rows, rows)

    queries = q_ref[...].reshape(groups * rows, 2 * HEAD) * jnp.asarray(0.125, BF16)
    grads = do_ref[...].reshape(groups * rows, 2 * HEAD)
    keyset = k_ref[...]
    valueset = v_ref[...]
    key_t = flip(keyset).astype(BF16)
    query_t = [flip(queries[g * rows : (g + 1) * rows]) for g in range(1, groups)]
    grad_t = [flip(grads[g * rows : (g + 1) * rows]) for g in range(1, groups)]
    own_key_t = [flip(ok_ref[g]) for g in range(groups - 1)]
    own_value_t = [flip(ov_ref[g]) for g in range(groups - 1)]
    dq_t, dok_t, dov_t = [], [], []
    place = lax.broadcasted_iota(jnp.int32, (rows, rows), 0)
    other = lax.broadcasted_iota(jnp.int32, (rows, rows), 1)
    reverse = (place + other == rows - 1).astype(F32).astype(BF16)
    dk = jnp.zeros((keys, 2 * HEAD), F32)
    dv = jnp.zeros((keys, 2 * HEAD), F32)
    for which in range(2):
        lo, hi = which * HEAD, (which + 1) * HEAD
        head_q = queries * head_mask(which)
        head_g = grads * head_mask(which)
        scores = dot_nt(keyset, head_q)
        grad_probs = dot_nt(valueset, head_g)
        bias = toeplitz(vec_ref, which, blocks, rows)
        bias_main = bias + mask_sc[0]
        bias_copy = bias + mask_sc[1]
        weights, grad_logits, dq_own, dok_h, dov_h = [], [], [], [], []
        own_sum = jnp.zeros((1, rows), F32)
        for g in range(groups):
            cols = slice(g * rows, (g + 1) * rows)
            lse = lse_ref[0, which : which + 1, cols]
            prob = jnp.exp(scores[:, cols] + (bias_main if g == 0 else bias_copy) - lse)
            grad_prob = grad_probs[:, cols]
            inner = jnp.sum(grad_prob * prob, axis=0, keepdims=True)
            if g:
                own_logit = (
                    jnp.sum(query_t[g - 1][lo:hi] * own_key_t[g - 1][lo:hi], axis=0, keepdims=True)
                    + own_bias_ref[2 * pair + which]
                )
                own_prob = jnp.exp(own_logit - lse)
                grad_own = jnp.sum(
                    grad_t[g - 1][lo:hi] * own_value_t[g - 1][lo:hi], axis=0, keepdims=True
                )
                inner = inner + grad_own * own_prob
                own_grad = (own_prob * (grad_own - inner)).astype(BF16).astype(F32)
                own_sum = own_sum + own_grad
                dq_own.append(own_grad * own_key_t[g - 1][lo:hi])
                dok_h.append(own_grad * query_t[g - 1][lo:hi])
                dov_h.append(own_prob.astype(BF16).astype(F32) * grad_t[g - 1][lo:hi])
            low = (prob * (grad_prob - inner)).astype(BF16)
            weights.append(prob.astype(BF16))
            grad_logits.append(low)
        low_all = jnp.concatenate(grad_logits, axis=1)
        dk = dk + dot_nn(low_all, head_q)
        dv = dv + dot_nn(jnp.concatenate(weights, axis=1), head_g)
        dq_h = dot_nn(key_t[lo:hi], low_all)
        dq_t.append(
            [
                (dq_h[:, g * rows : (g + 1) * rows] + (dq_own[g - 1] if g else 0.0)) * 0.125
                for g in range(groups)
            ]
        )
        dok_t.append(dok_h)
        dov_t.append(dov_h)
        own_ref[0, which : which + 1, :] = own_sum
        for block in range(blocks):
            turned = dot_nn(reverse, low_all[block * rows : (block + 1) * rows])
            part = turned[:, :rows]
            for g in range(1, groups):
                part = part + turned[:, g * rows : (g + 1) * rows]
            wide = jnp.concatenate([part, jnp.zeros_like(part)], axis=1)
            shifted = pltpu.roll(wide, rows + 1, axis=1, stride=1, stride_axis=0)
            diag_ref[0, which, block : block + 1, :] = jnp.sum(shifted, axis=0, keepdims=True)
    for g in range(groups):
        dq_ref[g] = jnp.concatenate([dq_t[0][g], dq_t[1][g]], axis=0).T.astype(BF16)
        if g:
            dok_ref[g - 1] = (
                jnp.concatenate([dok_t[0][g - 1], dok_t[1][g - 1]], axis=0).T.astype(BF16)
            )
            dov_ref[g - 1] = (
                jnp.concatenate([dov_t[0][g - 1], dov_t[1][g - 1]], axis=0).T.astype(BF16)
            )
    dk_ref[...] = dk.astype(BF16)
    dv_ref[...] = dv.astype(BF16)


def cross_mask(ends_ref, use_ref, mask_sc, blocks, rows):
    for block in range(blocks):
        same = segment_same(ends_ref, block, blocks, rows)[2]
        at = pl.ds(block * rows, rows)
        mask_sc[at, :] = jnp.where(same, use_ref[at, :], BIG)


def cross_fwd_kernel(ends_ref, q_ref, k_ref, v_ref, use_ref, out_ref, lse_ref, mask_sc):
    groups, rows, _ = q_ref.shape
    keys = k_ref.shape[0]
    pair = pl.program_id(0)

    @pl.when(pair == 0)
    def _():
        cross_mask(ends_ref, use_ref, mask_sc, keys // rows, rows)

    queries = q_ref[...].reshape(groups * rows, 2 * HEAD) * jnp.asarray(0.125, BF16)
    keyset = k_ref[...]
    value_t = flip(v_ref[...]).astype(BF16)
    outs = []
    for which in range(2):
        lo, hi = which * HEAD, (which + 1) * HEAD
        scores = dot_nt(keyset, queries * head_mask(which))
        head_out = []
        for g in range(groups):
            logit = scores[:, g * rows : (g + 1) * rows] + mask_sc[...]
            top = jnp.max(logit, axis=0, keepdims=True)
            expon = jnp.exp(logit - top)
            total = jnp.sum(expon, axis=0, keepdims=True)
            head_out.append(dot_nn(value_t[lo:hi], expon.astype(BF16)) / total)
            lse_ref[0, which : which + 1, g * rows : (g + 1) * rows] = top + jnp.log(total)
        outs.append(head_out)
    for g in range(groups):
        out_ref[g] = jnp.concatenate([outs[0][g], outs[1][g]], axis=0).T.astype(BF16)


def cross_bwd_kernel(
    ends_ref, q_ref, k_ref, v_ref, use_ref, lse_ref, do_ref, dq_ref, dk_ref, dv_ref, mask_sc
):
    groups, rows, _ = q_ref.shape
    keys = k_ref.shape[0]
    pair = pl.program_id(0)

    @pl.when(pair == 0)
    def _():
        cross_mask(ends_ref, use_ref, mask_sc, keys // rows, rows)

    queries = q_ref[...].reshape(groups * rows, 2 * HEAD) * jnp.asarray(0.125, BF16)
    grads = do_ref[...].reshape(groups * rows, 2 * HEAD)
    keyset = k_ref[...]
    valueset = v_ref[...]
    key_t = flip(keyset).astype(BF16)
    dk = jnp.zeros((keys, 2 * HEAD), F32)
    dv = jnp.zeros((keys, 2 * HEAD), F32)
    dq_t = []
    for which in range(2):
        lo, hi = which * HEAD, (which + 1) * HEAD
        head_q = queries * head_mask(which)
        head_g = grads * head_mask(which)
        scores = dot_nt(keyset, head_q)
        grad_probs = dot_nt(valueset, head_g)
        weights, grad_logits = [], []
        for g in range(groups):
            cols = slice(g * rows, (g + 1) * rows)
            prob = jnp.exp(scores[:, cols] + mask_sc[...] - lse_ref[0, which : which + 1, cols])
            grad_prob = grad_probs[:, cols]
            inner = jnp.sum(grad_prob * prob, axis=0, keepdims=True)
            weights.append(prob.astype(BF16))
            grad_logits.append((prob * (grad_prob - inner)).astype(BF16))
        low_all = jnp.concatenate(grad_logits, axis=1)
        dk = dk + dot_nn(low_all, head_q)
        dv = dv + dot_nn(jnp.concatenate(weights, axis=1), head_g)
        dq_t.append(dot_nn(key_t[lo:hi], low_all) * 0.125)
    for g in range(groups):
        cols = slice(g * rows, (g + 1) * rows)
        dq_ref[g] = jnp.concatenate([dq_t[0][:, cols], dq_t[1][:, cols]], axis=0).T.astype(BF16)
    dk_ref[...] = dk.astype(BF16)
    dv_ref[...] = dv.astype(BF16)


def slab(count, rows):
    return pl.BlockSpec((count, rows, 2 * HEAD), lambda i: (0, 0, i))


def column(rows):
    return pl.BlockSpec((rows, 2 * HEAD), lambda i: (0, i))


def pairwise(*dims):
    return pl.BlockSpec((1,) + dims, lambda i: (i,) + (0,) * len(dims))


SCALARS = pl.BlockSpec(memory_space=pltpu.SMEM)


def shape(*dims, kind=BF16):
    return jax.ShapeDtypeStruct(dims, kind)


def self_forward(ends, own_bias, queries, keyset, valueset, own_keys, own_values, vec):
    groups, rows, width = queries.shape
    keys = keyset.shape[0]
    pairs = width // (2 * HEAD)
    blocks = keys // rows
    return pl.pallas_call(
        self_fwd_kernel,
        grid=(pairs,),
        in_specs=[
            SCALARS,
            SCALARS,
            slab(groups, rows),
            column(keys),
            column(keys),
            slab(groups - 1, rows),
            slab(groups - 1, rows),
            pairwise(2, blocks, 2 * rows),
        ],
        out_specs=[slab(groups, rows), pairwise(2, groups * rows)],
        out_shape=[shape(groups, rows, width), shape(pairs, 2, groups * rows, kind=F32)],
        scratch_shapes=[pltpu.VMEM((2, keys, rows), F32)],
        name="self_forward",
    )(ends, own_bias, queries, keyset, valueset, own_keys, own_values, vec)


def self_backward(
    ends, own_bias, queries, keyset, valueset, own_keys, own_values, vec, lse, grad_out
):
    groups, rows, width = queries.shape
    keys = keyset.shape[0]
    pairs = width // (2 * HEAD)
    blocks = keys // rows
    return pl.pallas_call(
        self_bwd_kernel,
        grid=(pairs,),
        in_specs=[
            SCALARS,
            SCALARS,
            slab(groups, rows),
            column(keys),
            column(keys),
            slab(groups - 1, rows),
            slab(groups - 1, rows),
            pairwise(2, blocks, 2 * rows),
            pairwise(2, groups * rows),
            slab(groups, rows),
        ],
        out_specs=[
            slab(groups, rows),
            column(keys),
            column(keys),
            slab(groups - 1, rows),
            slab(groups - 1, rows),
            pairwise(2, blocks, 2 * rows),
            pairwise(2, rows),
        ],
        out_shape=[
            shape(groups, rows, width),
            shape(keys, width),
            shape(keys, width),
            shape(groups - 1, rows, width),
            shape(groups - 1, rows, width),
            shape(pairs, 2, blocks, 2 * rows, kind=F32),
            shape(pairs, 2, rows, kind=F32),
        ],
        scratch_shapes=[pltpu.VMEM((2, keys, rows), F32)],
        name="self_backward",
    )(ends, own_bias, queries, keyset, valueset, own_keys, own_values, vec, lse, grad_out)


def cross_forward(ends, queries, keyset, valueset, use):
    groups, rows, width = queries.shape
    keys = keyset.shape[0]
    pairs = width // (2 * HEAD)
    return pl.pallas_call(
        cross_fwd_kernel,
        grid=(pairs,),
        in_specs=[
            SCALARS,
            slab(groups, rows),
            column(keys),
            column(keys),
            pl.BlockSpec((keys, 1), lambda i: (0, 0)),
        ],
        out_specs=[slab(groups, rows), pairwise(2, groups * rows)],
        out_shape=[shape(groups, rows, width), shape(pairs, 2, groups * rows, kind=F32)],
        scratch_shapes=[pltpu.VMEM((keys, rows), F32)],
        name="cross_forward",
    )(ends, queries, keyset, valueset, use)


def cross_backward(ends, queries, keyset, valueset, use, lse, grad_out):
    groups, rows, width = queries.shape
    keys = keyset.shape[0]
    pairs = width // (2 * HEAD)
    return pl.pallas_call(
        cross_bwd_kernel,
        grid=(pairs,),
        in_specs=[
            SCALARS,
            slab(groups, rows),
            column(keys),
            column(keys),
            pl.BlockSpec((keys, 1), lambda i: (0, 0)),
            pairwise(2, groups * rows),
            slab(groups, rows),
        ],
        out_specs=[slab(groups, rows), column(keys), column(keys)],
        out_shape=[shape(groups, rows, width), shape(keys, width), shape(keys, width)],
        scratch_shapes=[pltpu.VMEM((keys, rows), F32)],
        name="cross_backward",
    )(ends, queries, keyset, valueset, use, lse, grad_out)


EPS = 1e-05
BUCKETS = 32


def product_kernel(where_ref, *refs, plan, lefts, rights, members, side_rows):
    left_refs = refs[:lefts]
    right_refs = refs[lefts : lefts + rights]
    outs = refs[lefts + rights : lefts + rights + 4]
    scratch = refs[lefts + rights + 4 :]
    step = pl.program_id(0)
    steps = pl.num_programs(0)
    half_width = outs[0].shape[-1]
    pair_at, core, member = where_ref[0], where_ref[1], where_ref[2]

    @pl.when(step == 0)
    def _():
        for number, pieces in enumerate(plan):
            for side in range(2):
                target = scratch[2 * number + side]
                base = 0
                for _, _, right, start, count in pieces:
                    for part in range(members):
                        source = ((part ^ member) * 2 + side) * half_width
                        target[base : base + count, part * half_width : (part + 1) * half_width] = (
                            right_refs[right][
                                start : start + count,
                                pl.ds(pl.multiple_of(source, 128), half_width),
                            ]
                        )
                    base += count

    order = ((2 * step + 1, 2 * step), (step + steps, step))
    for number, pieces in enumerate(plan):
        for side in range(2):
            columns = []
            for place in order[side]:
                block = ((place ^ pair_at) * 2 + core) * side_rows
                at = pl.ds(pl.multiple_of(block, 128), side_rows)
                columns.append(
                    jnp.concatenate(
                        [
                            left_refs[left][start : start + count, at]
                            for left, start, _, _, count in pieces
                        ],
                        axis=0,
                    )
                )
            result = lax.dot_general(
                jnp.concatenate(columns, axis=1),
                scratch[2 * number + side][...],
                (((0,), (0,)), ((), ())),
                preferred_element_type=F32,
            ).astype(BF16)
            for which in range(2):
                for part in range(members):
                    outs[2 * side + which][0, part, number * side_rows : (number + 1) * side_rows] = (
                        result[
                            which * side_rows : (which + 1) * side_rows,
                            part * half_width : (part + 1) * half_width,
                        ]
                    )


def products(where, lefts, rights, plan, dp, stream, name):
    weights = len(plan)
    side_rows = lefts[0].shape[1] // dp
    half_width = rights[0].shape[1] // (2 * stream)
    steps = dp // 4
    out = jax.ShapeDtypeStruct((steps, stream, weights * side_rows, half_width), BF16)
    scratch = []
    for pieces in plan:
        depth = sum(piece[4] for piece in pieces)
        scratch += [pltpu.VMEM((depth, stream * half_width), BF16)] * 2
    block = pl.BlockSpec(
        (1, stream, weights * side_rows, half_width), lambda i, where: (i, 0, 0, 0)
    )
    return pl.pallas_call(
        functools.partial(
            product_kernel,
            plan=plan,
            lefts=len(lefts),
            rights=len(rights),
            members=stream,
            side_rows=side_rows,
        ),
        grid_spec=pltpu.PrefetchScalarGridSpec(
            num_scalar_prefetch=1,
            grid=(steps,),
            in_specs=[
                pl.BlockSpec(array.shape, lambda i, where: (0, 0), pipeline_mode=pl.Buffered(1))
                for array in (*lefts, *rights)
            ],
            out_specs=[block] * 4,
            scratch_shapes=scratch,
        ),
        out_shape=[out] * 4,
        name=name,
    )(where, *lefts, *rights)


def swap(array, axis, bit, size):
    return lax.ppermute(array, axis, [(i, i ^ bit) for i in range(size)])


def add_up(terms):
    total = terms[0].astype(F32)
    for term in terms[1:]:
        total = total + term.astype(F32)
    return total


def reduce_blocks(parts, dp, stream):
    levels = (dp // 2).bit_length() - 1
    ends = []
    for side in range(2):
        send, keep = parts[2 * side], parts[2 * side + 1]
        order = list(range(levels)) if side == 0 else list(reversed(range(levels)))
        terms = [keep, swap(send, "dp", 2 << order[0], dp)]
        for level in order[1:]:
            halves = []
            for term in terms:
                count = term.shape[0] // 2
                split = (count, 2) if side == 0 else (2, count)
                term = term.reshape(split + term.shape[1:])
                halves.append((term[:, 0], term[:, 1]) if side == 0 else (term[0], term[1]))
            moved = add_up([half[1] for half in halves]).astype(BF16)
            terms = [half[0] for half in halves] + [swap(moved, "dp", 2 << level, dp)]
        ends.append(add_up(terms)[0])
    total = jnp.concatenate(ends, axis=-1)
    low = total.astype(BF16)
    result = total[0]
    for part in range(1, stream):
        result = result + swap(low[part], "stream", part, stream).astype(F32)
    return result


def norm_rows(resid, gain, shift):
    centre = jnp.mean(resid, axis=-1, keepdims=True)
    centred = resid - centre
    spread = jnp.mean(centred * centred, axis=-1, keepdims=True)
    return centred * lax.rsqrt(spread + EPS) * gain + shift


def gelu_exact(value):
    return jax.nn.gelu(value, approximate=False)


def matmul(left, right):
    return jnp.dot(left, right, preferred_element_type=F32)


def column_sum(array):
    return jnp.sum(array.astype(F32), axis=0)


def gather_members(array, stream):
    return jnp.concatenate(
        [array] + [swap(array, "stream", part, stream) for part in range(1, stream)], axis=0
    )


def scatter_members(array, rows, stream):
    low = array.astype(BF16)
    result = array[:rows]
    for part in range(1, stream):
        piece = low[part * rows : (part + 1) * rows]
        result = result + swap(piece, "stream", part, stream).astype(F32)
    return result


def local(
    main_states,
    predict_states,
    encoder_states,
    doc_lengths,
    encoder_keep,
    bucket_table,
    query_weight,
    key_weight,
    value_weight,
    out_weight,
    cross_query_weight,
    cross_key_weight,
    cross_value_weight,
    cross_out_weight,
    up_weight,
    down_weight,
    relative_bias,
    query_bias,
    value_bias,
    out_bias,
    cross_query_bias,
    cross_value_bias,
    cross_out_bias,
    up_bias,
    down_bias,
    norm_gain,
    norm_shift,
    main_cotangent,
    predict_cotangent,
    *,
    dp,
    stream,
):
    rows, width = main_states.shape
    copies = predict_states.shape[0]
    groups = copies + 1
    keys = rows * stream
    member = lax.axis_index("stream")
    index = lax.axis_index("dp")
    where = jnp.stack([index >> 1, index & 1, member]).astype(jnp.int32)
    core = functools.partial(swap, axis="dp", bit=1, size=dp)

    main_all = gather_members(main_states, stream)
    encoder_all = gather_members(encoder_states, stream)
    predict_rows = predict_states.reshape(copies * rows, width)
    all_rows = jnp.concatenate([main_states, predict_rows], axis=0)

    doc_ends = jnp.cumsum(doc_lengths[0])
    first = member * rows
    bases = (jnp.arange(stream, dtype=jnp.int32) ^ member) * rows
    ends = jnp.concatenate([doc_ends, first[None], bases]).astype(jnp.int32)
    places = jnp.arange(keys, dtype=jnp.int32)
    segment = jnp.sum((doc_ends[None, :] <= places[:, None]).astype(jnp.int32), axis=1)
    earlier = jnp.concatenate([jnp.full((1,), -1, jnp.int32), segment[:-1]])
    usable = ((encoder_keep > 0) | (segment != earlier)).reshape(stream, rows)
    usable = jnp.concatenate(
        [lax.dynamic_slice_in_dim(usable, part ^ member, 1) for part in range(stream)], axis=0
    )
    use = jnp.where(usable, 0.0, BIG).astype(F32).reshape(keys, 1)
    live_rows = ((first + jnp.arange(rows)) < doc_ends[-1]).astype(F32)

    offset = jnp.arange(2 * rows, dtype=jnp.int32)
    offset = jnp.where(offset < rows, offset, offset - 2 * rows)
    distance = jnp.clip(first + offset[None, :] - bases[:, None], 0, keys - 1)
    buckets = jnp.take(bucket_table, distance)
    onehot = (buckets[..., None] == jnp.arange(BUCKETS, dtype=jnp.int32)).astype(BF16)
    heads = width // HEAD
    vec = jnp.einsum("ajb,bh->haj", onehot, relative_bias, preferred_element_type=F32)
    vec = vec.reshape(heads // 2, 2, stream, 2 * rows)
    zero_hot = (jnp.arange(BUCKETS, dtype=jnp.int32) == bucket_table[0]).astype(BF16)
    own_bias = matmul(zero_hot[None, :], relative_bias)[0]

    query_low = (matmul(all_rows, query_weight) + query_bias).astype(BF16)
    own_keys = matmul(predict_rows, key_weight).astype(BF16).reshape(copies, rows, width)
    own_values = (matmul(predict_rows, value_weight) + value_bias).astype(BF16)
    own_values = own_values.reshape(copies, rows, width)
    keyset = matmul(main_all, key_weight).astype(BF16)
    valueset = (matmul(main_all, value_weight) + value_bias).astype(BF16)
    queries = query_low.reshape(groups, rows, width)
    attended, self_lse = self_forward(
        ends, own_bias, queries, keyset, valueset, own_keys, own_values, vec
    )
    ckeyset = matmul(encoder_all, cross_key_weight).astype(BF16)
    cvalueset = (matmul(encoder_all, cross_value_weight) + cross_value_bias).astype(BF16)
    attended_low = attended.reshape(groups * rows, width)
    first_sum = all_rows.astype(F32) + matmul(attended_low, out_weight) + out_bias
    hidden_one, norm_one_back = jax.vjp(norm_rows, first_sum, norm_gain[0], norm_shift[0])
    hidden_one_low = hidden_one.astype(BF16)
    cquery_low = (matmul(hidden_one_low, cross_query_weight) + cross_query_bias).astype(BF16)
    cqueries = cquery_low.reshape(groups, rows, width)
    cross_out, cross_lse = cross_forward(ends, cqueries, ckeyset, cvalueset, use)
    cross_low = cross_out.reshape(groups * rows, width)
    second_sum = hidden_one + matmul(cross_low, cross_out_weight) + cross_out_bias
    hidden_two, norm_two_back = jax.vjp(norm_rows, second_sum, norm_gain[1], norm_shift[1])
    hidden_two_low = hidden_two.astype(BF16)
    inner_pre = matmul(hidden_two_low, up_weight) + up_bias
    activated, gelu_back = jax.vjp(gelu_exact, inner_pre)
    activated_low = activated.astype(BF16)
    third_sum = hidden_two + matmul(activated_low, down_weight) + down_bias
    result, norm_three_back = jax.vjp(norm_rows, third_sum, norm_gain[2], norm_shift[2])
    main_out = result[:rows].astype(BF16)
    predict_out = result[rows:].reshape(copies, rows, width).astype(BF16)

    main_far, predict_far, encoder_far = core(main_all), core(predict_rows), core(encoder_all)
    attended_far, one_far = core(attended_low), core(hidden_one_low)
    cross_far, two_far, activated_far = core(cross_low), core(hidden_two_low), core(activated_low)

    def reduced(lefts, rights, plan, name):
        parts = products(where, lefts, rights, plan, dp, stream, name)
        return reduce_blocks(parts, dp, stream)

    count = groups * rows

    def paired(left, right):
        return ((left, 0, right, 0, count), (left + 1, 0, right + 1, 0, count))

    cotangent = jnp.concatenate([main_cotangent[None], predict_cotangent], axis=0)
    cotangent = cotangent.reshape(count, width).astype(F32) * jnp.tile(live_rows, groups)[:, None]
    third_grad, gain_three, shift_three = norm_three_back(cotangent)
    ffn_grad = third_grad.astype(BF16)
    down_grad = reduced(
        (activated_low, activated_far), (ffn_grad, core(ffn_grad)), (paired(0, 0),), "down_products"
    )
    act_grad = right_inner(ffn_grad, down_weight)
    inner_grad = gelu_back(act_grad)[0].astype(BF16)
    up_grad = reduced(
        (hidden_two_low, two_far), (inner_grad, core(inner_grad)), (paired(0, 0),), "up_products"
    )
    two_grad = third_grad + right_inner(inner_grad, up_weight)
    second_grad, gain_two, shift_two = norm_two_back(two_grad)
    branch_two = second_grad.astype(BF16)
    cross_attended_grad = right_inner(branch_two, cross_out_weight).astype(BF16)
    cquery_part, ckey_part, cvalue_part = cross_backward(
        ends,
        cqueries,
        ckeyset,
        cvalueset,
        use,
        cross_lse,
        cross_attended_grad.reshape(groups, rows, width),
    )
    cquery_grad = cquery_part.reshape(count, width)
    cross_grads = reduced(
        (cross_low, cross_far, hidden_one_low, one_far),
        (branch_two, core(branch_two), cquery_grad, core(cquery_grad)),
        (paired(0, 0), paired(2, 2)),
        "cross_products",
    )
    encoder_plan = tuple(
        ((0, 0, right, 0, keys), (1, 0, right + 1, 0, keys)) for right in (0, 2)
    )
    encoder_grads = reduced(
        (encoder_all, encoder_far),
        (ckey_part, core(ckey_part), cvalue_part, core(cvalue_part)),
        encoder_plan,
        "encoder_products",
    )
    encoder_part = right_inner(ckey_part, cross_key_weight) + right_inner(
        cvalue_part, cross_value_weight
    )
    encoder_grad = scatter_members(encoder_part, rows, stream).astype(BF16)
    one_grad = second_grad + right_inner(cquery_grad, cross_query_weight)
    first_grad, gain_one, shift_one = norm_one_back(one_grad)
    branch_one = first_grad.astype(BF16)
    out_grad = reduced(
        (attended_low, attended_far), (branch_one, core(branch_one)), (paired(0, 0),), "out_products"
    )
    attended_grad = right_inner(branch_one, out_weight).astype(BF16)
    query_part, key_part, value_part, own_key_grad, own_value_grad, diag, own_sums = self_backward(
        ends,
        own_bias,
        queries,
        keyset,
        valueset,
        own_keys,
        own_values,
        vec,
        self_lse,
        attended_grad.reshape(groups, rows, width),
    )
    query_grad = query_part.reshape(count, width)
    own_key_grad = own_key_grad.reshape(copies * rows, width)
    own_value_grad = own_value_grad.reshape(copies * rows, width)
    rights = (query_grad, key_part, own_key_grad, value_part, own_value_grad)
    rights = rights + tuple(core(right) for right in rights)
    copy_rows = copies * rows
    self_plan = (
        (
            (0, 0, 0, 0, rows),
            (1, 0, 0, rows, copy_rows),
            (2, 0, 5, 0, rows),
            (3, 0, 5, rows, copy_rows),
        ),
        (
            (0, 0, 1, 0, keys),
            (1, 0, 2, 0, copy_rows),
            (2, 0, 6, 0, keys),
            (3, 0, 7, 0, copy_rows),
        ),
        (
            (0, 0, 3, 0, keys),
            (1, 0, 4, 0, copy_rows),
            (2, 0, 8, 0, keys),
            (3, 0, 9, 0, copy_rows),
        ),
    )
    self_grads = reduced(
        (main_all, predict_rows, main_far, predict_far), rights, self_plan, "self_products"
    )
    main_part = right_inner(key_part, key_weight) + right_inner(value_part, value_weight)
    row_grad = first_grad + right_inner(query_grad, query_weight)
    main_grad = (row_grad[:rows] + scatter_members(main_part, rows, stream)).astype(BF16)
    predict_grad = (
        row_grad[rows:]
        + right_inner(own_key_grad, key_weight)
        + right_inner(own_value_grad, value_weight)
    )
    predict_grad = predict_grad.reshape(copies, rows, width).astype(BF16)

    relative_grad = jnp.einsum(
        "haj,ajb->bh",
        diag.reshape(heads, stream, 2 * rows),
        onehot.astype(F32),
        precision=lax.Precision.HIGHEST,
    )
    relative_grad = (
        relative_grad
        + zero_hot.astype(F32)[:, None] * jnp.sum(own_sums.reshape(heads, rows), axis=1)[None, :]
    )
    small = jnp.concatenate(
        [
            column_sum(query_grad),
            column_sum(value_part) + column_sum(own_value_grad),
            column_sum(branch_one),
            column_sum(cquery_grad),
            column_sum(cvalue_part),
            column_sum(branch_two),
            column_sum(inner_grad),
            column_sum(ffn_grad),
            gain_one,
            gain_two,
            gain_three,
            shift_one,
            shift_two,
            shift_three,
            relative_grad.reshape(-1),
        ]
    )
    small = jnp.concatenate([small, jnp.zeros((-small.shape[0] % 1024,), F32)]).reshape(-1, 1024)
    bit = 1
    while bit < dp:
        small = small + swap(small, "dp", bit, dp)
        bit *= 2
    bit = 1
    while bit < stream:
        small = small + swap(small, "stream", bit, stream)
        bit *= 2
    small = small.reshape(-1)
    sizes = [width] * 6 + [up_bias.shape[0]] + [width] * 7 + [BUCKETS * heads]
    pieces, at = [], 0
    for size in sizes:
        pieces.append(small[at : at + size])
        at += size
    side = width // dp
    return (
        main_out,
        predict_out,
        main_grad,
        predict_grad,
        encoder_grad,
        self_grads[:side],
        self_grads[side : 2 * side],
        self_grads[2 * side :],
        out_grad,
        cross_grads[side:],
        encoder_grads[:side],
        encoder_grads[side:],
        cross_grads[:side],
        up_grad,
        down_grad,
        pieces[14].reshape(BUCKETS, heads),
        pieces[0],
        pieces[1],
        pieces[2],
        pieces[3],
        pieces[4],
        pieces[5],
        pieces[6],
        pieces[7],
        jnp.stack(pieces[8:11]),
        jnp.stack(pieces[11:14]),
    )


def right_inner(left, right):
    return dot_nt(left, right)


def solution(mesh):
    body = functools.partial(local, dp=mesh.shape["dp"], stream=mesh.shape["stream"])
    rows = P(("dp", "stream"), None)
    copies = P(None, ("dp", "stream"), None)
    return jax.shard_map(
        body,
        mesh=mesh,
        in_specs=(rows, copies, rows, P("dp", None), P("dp"))
        + (P(),) * 22
        + (rows, copies),
        out_specs=(rows, copies, rows, copies, rows)
        + (P("dp", "stream"),) * 10
        + (P(),) * 11,
        check_vma=False,
    )
```
